32 devices in a mesh: groups: 2 (over x), zonal: 16 (over z, y, core).
Axes of the slice: x: 2, y: 2, z: 4, core: 2. Of those that a mesh axis runs over, the one named last changes fastest.
Arguments:
- field: bfloat16 [192, 32, 2048], P('groups', None, 'zonal'), parts along dimension 0, may hold values from -6 to 6
- land_mask: int32 [32, 2048], P(None, 'zonal'), may hold values from 0 to 1, as said below
- dw_weight: float32 [2, 49, 96], replicated, may hold values from -0.875 to 0.875
- ln_gain: float32 [2, 96], replicated, may hold values from 0.1 to 1.9
- ln_shift: float32 [2, 96], replicated, may hold values from -3 to 3
- w_in: bfloat16 [2, 384, 96], replicated, may hold values from -0.625 to 0.625
- b_in: float32 [2, 384], replicated, may hold values from -3 to 3
- w_out: bfloat16 [2, 96, 384], replicated, may hold values from -0.3125 to 0.3125
Outputs:
- evolved: bfloat16 [192, 32, 2048], P('groups', None, 'zonal'), parts along dimension 0
The draws below stay inside these ranges and needn't reach their ends.
There are 2 independent parts, one for each index of `groups`. The reference program is written for one: setup_inputs(seed, part) draws one part's arguments, and reference() takes and returns one part's arrays. A program takes and returns all parts, laid end to end along the dimension named above; an argument that names none is the same for every part. Nothing has to cross between parts.
Inputs may be any that keep to these rules, and one draw needn't show every extreme that they name: `land_mask`: 1 marks an ocean cell, 0 a land cell.
All inputs are finite; a program needn't handle non-finite values.
Results may differ from the reference program's by a relative error of at most 0.0058.
Values may be sent and summed in bfloat16 or wider, within the bound.
A program may use at most 64 MiB of HBM per device.

```python
import jax
import jax.numpy as jnp
from jax import lax

C = 96
H = 384
BLOCKS = 2
ROWS = 32
CX = 128
NX = 2048


def draw_land_mask(key, part):
    key_tile = jax.random.fold_in(key, 11)
    key_cell = jax.random.fold_in(key, 23)
    tile_land = jax.random.randint(key_tile, (ROWS // 32, NX // CX), 0, 3) == 0
    cell_land = jax.random.randint(key_cell, (ROWS, NX), 0, 8) == 0
    blocks = jnp.repeat(jnp.repeat(tile_land, 32, axis=0), CX, axis=1)
    ocean = jnp.logical_not(jnp.logical_or(blocks, cell_land))
    return ocean.astype(jnp.int32)


def steps_of(rng, dims, cuts, low, top_value):
    def one(dim, shards_of):
        heights = jax.random.uniform(jax.random.fold_in(jax.random.fold_in(rng, 6), dim), (shards_of,), jnp.float32, low / len(cuts), top_value / len(cuts))
        return jnp.repeat(jnp.exp(heights), dims[dim] // shards_of).reshape((-1,) + (1,) * (len(dims) - dim - 1))

    level = one(*cuts[0])
    for cut in cuts[1:]:
        level = level * one(*cut)
    return level


def centred(own_key, extent, spread, bound, split=(), kind=jnp.bfloat16):
    entries = spread * jax.random.normal(own_key, extent, jnp.float32)
    if split:
        entries = entries * steps_of(own_key, extent, split, -0.22, 0.18)
    return jnp.clip(entries, -bound, bound).astype(kind)


def setup_inputs(seed: int = 0, part: int = 0) -> dict:
    key_list = jax.random.split(jax.random.key(seed), 9)
    own_keys = jax.random.split(jax.random.fold_in(key_list[8], part), 9)
    field = centred(own_keys[0], (C, ROWS, NX), 1.0, 6.0, ((2, 16),))
    land_mask = draw_land_mask(jax.random.fold_in(key_list[8], 71), part)
    dw_weight = centred(key_list[2], (BLOCKS, 49, C), 49 ** -0.5, 0.875, (), jnp.float32)
    ln_gain = jnp.clip(1.0 + 0.18 * jax.random.normal(key_list[3], (BLOCKS, C), jnp.float32), 0.1, 1.9)
    ln_shift = centred(key_list[4], (BLOCKS, C), 0.5, 3.0, (), jnp.float32)
    w_in = centred(key_list[5], (BLOCKS, H, C), C ** -0.5, 0.625)
    b_in = centred(key_list[6], (BLOCKS, H), 0.5, 3.0, (), jnp.float32)
    w_out = centred(key_list[7], (BLOCKS, C, H), H ** -0.5, 0.3125)
    return {"field": field, "land_mask": land_mask, "dw_weight": dw_weight, "ln_gain": ln_gain, "ln_shift": ln_shift, "w_in": w_in, "b_in": b_in, "w_out": w_out}


def pad_state(state):
    ext = jnp.concatenate([state[:, :, -3:], state, state[:, :, :3]], axis=2)
    north = ext[:, -3:, ::-1][:, ::-1, :]
    south = jnp.zeros((state.shape[0], 3, ext.shape[2]), state.dtype)
    return jnp.concatenate([south, ext, north], axis=1)

def reference(field, land_mask, dw_weight, ln_gain, ln_shift, w_in, b_in, w_out):
    mask_b = land_mask.astype(jnp.bfloat16)
    state = field * mask_b[None]
    for blk in range(BLOCKS):
        padded = pad_state(state)
        conv = jnp.zeros(state.shape, jnp.float32)
        for p in range(7):
            for q in range(7):
                conv = conv + dw_weight[blk, 7 * p + q][:, None, None] * padded[:, p:p + ROWS, q:q + NX]
        gain = ln_gain[blk]
        shift = ln_shift[blk]
        wa = w_in[blk]
        ba = b_in[blk]
        wb = w_out[blk]

        def rowblock(index, out):
            start = (index * 32).astype(jnp.int32)
            yb = lax.dynamic_slice_in_dim(conv, start, 32, 1)
            xb = lax.dynamic_slice_in_dim(state, start, 32, 1)
            mb = lax.dynamic_slice_in_dim(land_mask, start, 32, 0)
            mean = lax.optimization_barrier(jnp.mean(yb, axis=0))
            cent = yb - mean
            var = lax.optimization_barrier(jnp.mean(cent * cent, axis=0))
            normed = (cent * lax.rsqrt(var + 1e-06) * gain[:, None, None] + shift[:, None, None]).astype(jnp.bfloat16)
            flat = normed.reshape(normed.shape[0], -1)
            hidden = jnp.dot(wa, flat, preferred_element_type=jnp.float32) + ba[:, None]
            hidden = jax.nn.gelu(hidden, approximate=True).astype(jnp.bfloat16)
            outer = jnp.dot(wb, hidden, preferred_element_type=jnp.float32).reshape(yb.shape)
            res = (mb.astype(jnp.float32)[None] * (xb.astype(jnp.float32) + outer)).astype(jnp.bfloat16)
            return lax.dynamic_update_slice_in_dim(out, res, start, 1)
        state = lax.fori_loop(0, ROWS // 32, rowblock, jnp.zeros(state.shape, jnp.bfloat16))
    return state
```

```python
import functools

import jax
import jax.numpy as jnp
from jax import lax
from jax.experimental import pallas as pl
from jax.experimental.pallas import tpu as pltpu
from jax.sharding import PartitionSpec as P

F32 = jnp.float32
BF16 = jnp.bfloat16
GROUP = 8
FOLD = 6
PAD = 1
STEP = 16
PAIRS = 24
K0 = 0.7978845608028654
K1 = K0 * 0.044715


def roll(x, shift):
    return pltpu.roll(x, shift % x.shape[-1], axis=x.ndim - 1)


def lanes_of(shape):
    return lax.broadcasted_iota(jnp.int32, shape, len(shape) - 1)


def rows_of(shape):
    return lax.broadcasted_iota(jnp.int32, shape, len(shape) - 2)


def shifted(cells, halo, lane, d):
    width = cells.shape[-1]
    if d == 0:
        return cells
    beyond = lane < d if d > 0 else lane >= width + d
    return roll(jnp.where(beyond, halo, cells), -d)


def kernel(
    n, field_hbm, mask_hbm, dw_hbm, gain_hbm, shift_hbm, wa_hbm, ba_hbm, wb_hbm, out_ref,
    field_ref, mask_ref, dw_ref, gain_ref, shift_ref, wa_ref, ba_ref, wb_ref,
    state, conv, t_low, t_high, pack, top, edge, west, east, ftop, feast, fwest, expand,
    contract, gains, shifts, moved_ref, side_w, north_w, loads, send, recv,
):
    channels, rows, width = field_ref.shape
    taps, blocks = dw_ref.shape[:2]
    hidden_units = wa_ref.shape[2]
    tiles = pack.shape[1]
    groups = width // GROUP
    deep = edge.shape[1]
    pitch = rows + PAD
    lane = lanes_of((rows, width))
    lane_c = lanes_of((channels, width))
    lane_e = lanes_of((deep, width))

    me = lax.axis_index("zonal")
    right, left = lax.rem(me + 1, n), lax.rem(me + n - 1, n)
    across = n - 1 - me
    a_east, a_west = lax.rem(across + 1, n), lax.rem(across + n - 1, n)
    barrier = pltpu.get_barrier_semaphore()

    def greet(device):
        pl.semaphore_signal(
            barrier, inc=1, device_id={"zonal": device}, device_id_type=pl.DeviceIdType.MESH
        )

    for device in (right, left, across):
        greet(device)

    @pl.when(a_east != me)
    def _():
        greet(a_east)

    @pl.when(a_west != me)
    def _():
        greet(a_west)

    def load(tile):
        at = pl.ds(tile * groups, groups)
        return pltpu.make_async_copy(field_hbm.at[at], field_ref.at[at], loads.at[tile])

    small = [
        pltpu.make_async_copy(src, dst, loads.at[tiles + i])
        for i, (src, dst) in enumerate(
            (
                (mask_hbm, mask_ref),
                (dw_hbm, dw_ref),
                (gain_hbm, gain_ref),
                (shift_hbm, shift_ref),
                (wa_hbm, wa_ref),
                (ba_hbm, ba_ref),
                (wb_hbm, wb_ref),
            )
        )
    ]
    small[0].start()
    for tile in range(tiles):
        load(tile).start()
    for each in small[1:]:
        each.start()

    def copy(src, dst, block, slot, device):
        return pltpu.make_async_remote_copy(
            src_ref=src.at[block],
            dst_ref=dst.at[block],
            send_sem=send.at[block, slot],
            recv_sem=recv.at[block, slot],
            device_id={"zonal": device},
            device_id_type=pl.DeviceIdType.MESH,
        )

    def sides(block):
        return copy(pack, west, block, 0, right), copy(pack, east, block, 1, left)

    def fold(block, act):
        for slot, device, dst in ((3, a_east, feast), (4, a_west, fwest)):

            @pl.when(device != me)
            def _():
                act(copy(edge, dst, block, slot, device))

            @pl.when(device == me)
            def _():
                act(
                    pltpu.make_async_copy(
                        edge.at[block], dst.at[block], recv.at[block, slot]
                    )
                )

        act(copy(top, ftop, block, 2, across))

    def row(r):
        return pl.ds(r, channels, stride=pitch)

    def channel(c):
        return pl.ds(c * pitch, rows)

    def pack_top(block):
        acc = jnp.zeros((deep, width), F32)
        for k in range(3):
            cells = state[row(rows - 1 - k), :]
            top[block, k] = cells.astype(BF16)
            for part in range(channels // deep):
                at = (k * (channels // deep) + part) * FOLD
                inside = (lane_e >= at) & (lane_e < at + FOLD)
                acc = jnp.where(inside, roll(cells[part * deep : (part + 1) * deep], at + 3), acc)
        edge[block] = acc.astype(BF16)

    def pack_side(block, tile, each):
        acc = jnp.zeros((rows, width), F32)
        for g in range(groups):
            inside = (lane >= g * GROUP) & (lane < (g + 1) * GROUP)
            acc = jnp.where(inside, roll(each(tile * groups + g), g * GROUP + 3), acc)
        pack[block, tile] = acc.astype(BF16)

    def send_all(block):
        for each in sides(block):
            each.start()
        fold(block, lambda c: c.start())

    def columns(values):
        size = values.shape[1]
        return jnp.transpose(jnp.broadcast_to(values, (width, size)))

    def prepare(block):
        gains[...] = columns(gain_ref[block : block + 1])
        shifts[...] = columns(shift_ref[block : block + 1])
        bias = ba_ref[block : block + 1]
        high = bias.astype(BF16).astype(F32)
        extra = expand.shape[1] - channels
        at = rows_of((extra, hidden_units))
        tail = jnp.where(at == 0, high, jnp.where(at == 1, bias - high, 0.0)).astype(BF16)
        expand[...] = jnp.transpose(jnp.concatenate([wa_ref[block], tail], axis=0))
        contract[...] = wb_ref[block] * jnp.asarray(0.5, BF16)

    def bands(block):
        weights = jnp.transpose(dw_ref[:, block, :])
        tap = lax.broadcasted_iota(jnp.int32, (taps, 2 * width), 0)
        col = lax.broadcasted_iota(jnp.int32, (taps, 2 * width), 1)
        p, q = tap // 7, tap % 7
        hit = jnp.where(col // rows == q, col % rows + 3 - p, -1)
        narrow = weights.astype(BF16)
        for r in range(rows):
            pick = jnp.where(hit == r, 1.0, 0.0).astype(BF16)
            band = jnp.dot(narrow, pick, preferred_element_type=F32)
            t_low[row(r), :] = band[:, :width]
            t_high[row(r), :] = band[:, width:]

    def edge_weights(block):
        weights = dw_ref[:, block, :]
        spread = jnp.where(
            lanes_of((channels, tiles * width)) // GROUP == rows_of((channels, tiles * width)), 1.0, 0.0
        ).astype(BF16)
        wide = jnp.dot(weights.astype(BF16), spread, preferred_element_type=F32)
        slot = lanes_of((1, tiles * width)) % GROUP
        for p in range(7):
            for s in range(1, 4):
                low = jnp.where((slot < 3) & (slot + s >= 3), wide[7 * p + 3 + s : 7 * p + 4 + s], 0.0)
                high = jnp.where(
                    (slot >= 3) & (slot < 6) & (slot - s < 3), wide[7 * p + 3 - s : 7 * p + 4 - s], 0.0
                )
                side_w[3 * p + s - 1 : 3 * p + s, :] = low + high
        turned = jnp.transpose(weights)
        for i in range(21):
            north_w[i] = jnp.broadcast_to(turned[:, 28 + i : 29 + i], (channels, width))

    def convolve():
        def parts(c):
            cells = state[channel(c), :]
            return jnp.concatenate(
                [(cells if j == 3 else roll(cells, 3 - j)).astype(BF16) for j in range(7)], axis=0
            )

        def band(c):
            at = channel(c)
            return jnp.concatenate([t_low[at, :], t_high[at, :]], axis=1).astype(BF16)[:, : 7 * rows]

        @pl.loop(0, channels // (2 * PAIRS))
        def _(index):
            for i in range(PAIRS):
                c = index * (2 * PAIRS) + 2 * i
                both = jnp.dot(
                    jnp.concatenate([band(c), band(c + 1)], axis=0),
                    jnp.concatenate([parts(c), parts(c + 1)], axis=1),
                    preferred_element_type=F32,
                )
                conv[channel(c), :] = both[:rows, :width]
                conv[channel(c + 1), :] = both[rows:, width:]

    def correct(block):
        slot = lane % GROUP
        outer = (lane < 3) | (lane >= width - 3)
        for tile in range(tiles):
            diff = jnp.where(
                slot >= 3, east[block, tile].astype(F32), west[block, tile].astype(F32)
            ) - pack[block, tile].astype(F32)
            for s in range(1, 4):
                moved_ref[s - 1, tile, pl.ds(8, rows), :] = jnp.where(
                    slot < 3, roll(diff, -s), roll(diff, s)
                )
            total = jnp.zeros((rows, width), F32)
            for p in range(7):
                for s in range(1, 4):
                    total = total + (
                        side_w[3 * p + s - 1 : 3 * p + s, tile * width : (tile + 1) * width]
                        * moved_ref[s - 1, tile, pl.ds(5 + p, rows), :]
                    )
            for g in range(groups):
                at = channel(tile * groups + g)
                conv[at, :] += jnp.where(outer, roll(total, -(g * GROUP + 3)), 0.0)

    def add_north(block):
        flip = jnp.where(
            rows_of((width, width)) + lanes_of((width, width)) == width - 1, 1.0, 0.0
        ).astype(BF16)
        both = jnp.where(
            lane_e % FOLD >= 3, feast[block].astype(F32), fwest[block].astype(F32)
        )
        sums = [conv[row(rows - 3 + r), :] for r in range(3)]
        for k in range(3):
            parts = [
                roll(both, -((k * (channels // deep) + part) * FOLD + 3))
                for part in range(channels // deep)
            ]
            halo = jnp.dot(
                jnp.concatenate(parts, axis=0).astype(BF16), flip, preferred_element_type=F32
            )
            cells = jnp.dot(ftop[block, k], flip, preferred_element_type=F32)
            for q in range(7):
                moved = shifted(cells, halo, lane_c, q - 3)
                for r in range(k, 3):
                    sums[r] = sums[r] + north_w[7 * (2 + k - r) + q] * moved
        for r in range(3):
            conv[row(rows - 3 + r), :] = sums[r]

    def mlp(start, step):
        extra = expand.shape[1] - channels
        ones = jnp.where(rows_of((extra, width)) < 2, 1.0, 0.0).astype(BF16)
        normed = []
        for k in range(step):
            y = conv[row(start + k), :]
            mean = jnp.sum(y, axis=0, keepdims=True) * (1.0 / channels)
            cent = y - mean
            var = jnp.sum(cent * cent, axis=0, keepdims=True) * (1.0 / channels)
            unit = (cent * lax.rsqrt(var + 1e-06) * gains[...] + shifts[...]).astype(BF16)
            normed.append(jnp.concatenate([unit, ones], axis=0))
        v = jnp.dot(
            expand[...], jnp.concatenate(normed, axis=1), preferred_element_type=F32
        ).astype(BF16)
        th = jnp.tanh(v * (jnp.asarray(K0, BF16) + jnp.asarray(K1, BF16) * (v * v)))
        outer = jnp.dot(contract[...], v + v * th, preferred_element_type=F32)
        for k in range(step):
            keep = mask_ref[pl.ds(start + k, 1), :].astype(F32)
            res = keep * (state[row(start + k), :] + outer[:, k * width : (k + 1) * width])
            state[row(start + k), :] = res.astype(BF16).astype(F32)

    moved_ref[...] = jnp.zeros(moved_ref.shape, F32)
    small[0].wait()
    maskf = mask_ref[...].astype(F32)
    for tile in range(tiles):
        load(tile).wait()

        def masked(c):
            cells = field_ref[c].astype(F32) * maskf
            state[channel(c), :] = cells
            return cells

        pack_side(0, tile, masked)

    pack_top(0)
    alone = jnp.where(a_east == me, 1, 0) + jnp.where(a_west == me, 1, 0)
    pl.semaphore_wait(barrier, 5 - alone)
    send_all(0)
    for each in small[1:]:
        each.wait()

    for block in range(blocks):
        bands(block)
        edge_weights(block)
        convolve()
        prepare(block)
        for each in sides(block):
            each.wait()
        correct(block)
        for start in range(0, rows - STEP, STEP):
            mlp(start, STEP)
        fold(block, lambda c: c.wait())
        add_north(block)
        mlp(rows - STEP, STEP)

        if block < blocks - 1:
            for tile in range(tiles):
                pack_side(block + 1, tile, lambda c: state[channel(c), :])
            pack_top(block + 1)
            send_all(block + 1)

    for c in range(channels):
        out_ref[c] = state[channel(c), :].astype(BF16)


VMEM = pl.BlockSpec(memory_space=pltpu.VMEM)
HBM = pl.BlockSpec(memory_space=pltpu.HBM)


def local(field, land_mask, dw_weight, ln_gain, ln_shift, w_in, b_in, w_out):
    channels, rows, width = field.shape
    blocks = dw_weight.shape[0]
    tiles = channels * GROUP // width
    hidden = w_in.shape[1]
    flat = pltpu.VMEM((channels * (rows + PAD), width), F32)
    packed = pltpu.VMEM((blocks, tiles, rows, width), BF16)
    tops = pltpu.VMEM((blocks, 3, channels, width), BF16)
    edges = pltpu.VMEM((blocks, 16, width), BF16)
    wide = pltpu.VMEM((channels, width), F32)
    args = (
        field,
        land_mask,
        jnp.swapaxes(dw_weight, 0, 1),
        ln_gain,
        ln_shift,
        jnp.swapaxes(w_in, 1, 2),
        b_in,
        w_out,
    )
    return pl.pallas_call(
        functools.partial(kernel, lax.axis_size("zonal")),
        out_shape=jax.ShapeDtypeStruct(field.shape, BF16),
        in_specs=[HBM] * 8,
        out_specs=VMEM,
        scratch_shapes=[pltpu.VMEM(a.shape, a.dtype) for a in args]
        + [
            flat,
            flat,
            flat,
            flat,
            packed,
            tops,
            edges,
            packed,
            packed,
            tops,
            edges,
            edges,
            pltpu.VMEM((hidden, channels + 16), BF16),
            pltpu.VMEM((channels, hidden), BF16),
            wide,
            wide,
            pltpu.VMEM((3, tiles, rows + 16, width), F32),
            pltpu.VMEM((24, tiles * width), F32),
            pltpu.VMEM((21, channels, width), F32),
            pltpu.SemaphoreType.DMA((tiles + 7,)),
            pltpu.SemaphoreType.DMA((blocks, 5)),
            pltpu.SemaphoreType.DMA((blocks, 5)),
        ],
        compiler_params=pltpu.CompilerParams(
            collective_id=0, has_side_effects=True, vmem_limit_bytes=60 * 1024 * 1024
        ),
        name="evolve",
    )(*args)


def solution(mesh):
    placed = (P("groups", None, "zonal"), P(None, "zonal"), P(), P(), P(), P(), P(), P())
    return jax.shard_map(
        local, mesh=mesh, in_specs=placed, out_specs=P("groups", None, "zonal"), check_vma=False
    )
```

```python
import functools

import jax
import jax.numpy as jnp
from jax import lax
from jax.experimental import pallas as pl
from jax.experimental.pallas import tpu as pltpu
from jax.sharding import PartitionSpec as P

F32 = jnp.float32
BF16 = jnp.bfloat16
GROUP = 8
FOLD = 6
PAD = 1
PAIRS = 24
K0 = 0.7978845608028654
K1 = K0 * 0.044715


def roll(x, shift):
    return pltpu.roll(x, shift % x.shape[-1], axis=x.ndim - 1)


def lanes_of(shape):
    return lax.broadcasted_iota(jnp.int32, shape, len(shape) - 1)


def rows_of(shape):
    return lax.broadcasted_iota(jnp.int32, shape, len(shape) - 2)


def shifted(cells, halo, lane, d):
    width = cells.shape[-1]
    if d == 0:
        return cells
    beyond = lane < d if d > 0 else lane >= width + d
    return roll(jnp.where(beyond, halo, cells), -d)


def kernel(
    n, field_hbm, mask_hbm, dw_hbm, gain_hbm, shift_hbm, wa_hbm, ba_hbm, wb_hbm, state,
    field_ref, mask_ref, dw_ref, gain_ref, shift_ref, wa_ref, ba_ref, wb_ref,
    conv, t_low, t_high, pack, top, edge, west, east, ftop, feast, fwest, expand,
    contract, gains, shifts, moved_ref, side_w, north_w, loads, send, recv,
):
    channels, rows, width = field_ref.shape
    taps, blocks = dw_ref.shape[:2]
    hidden_units = wa_ref.shape[2]
    tiles = pack.shape[2]
    groups = width // GROUP
    deep = edge.shape[1]
    pitch = rows + PAD
    lane = lanes_of((rows, width))
    lane_c = lanes_of((channels, width))
    lane_e = lanes_of((deep, width))

    me = lax.axis_index("zonal")
    right, left = lax.rem(me + 1, n), lax.rem(me + n - 1, n)
    across = n - 1 - me
    a_east, a_west = lax.rem(across + 1, n), lax.rem(across + n - 1, n)
    barrier = pltpu.get_barrier_semaphore()

    def greet(device):
        pl.semaphore_signal(
            barrier, inc=1, device_id={"zonal": device}, device_id_type=pl.DeviceIdType.MESH
        )

    for device in (right, left, across):
        greet(device)

    @pl.when(a_east != me)
    def _():
        greet(a_east)

    @pl.when(a_west != me)
    def _():
        greet(a_west)

    def load(tile):
        at = pl.ds(tile * groups, groups)
        return pltpu.make_async_copy(field_hbm.at[at], field_ref.at[at], loads.at[tile])

    small = [
        pltpu.make_async_copy(src, dst, loads.at[tiles + i])
        for i, (src, dst) in enumerate(
            (
                (mask_hbm, mask_ref),
                (dw_hbm, dw_ref),
                (gain_hbm, gain_ref),
                (shift_hbm, shift_ref),
                (wa_hbm, wa_ref),
                (ba_hbm, ba_ref),
                (wb_hbm, wb_ref),
            )
        )
    ]
    small[0].start()
    for tile in range(tiles):
        load(tile).start()
    for each in small[1:]:
        each.start()

    def copy(src, dst, block, slot, device):
        return pltpu.make_async_remote_copy(
            src_ref=src.at[block],
            dst_ref=dst.at[block],
            send_sem=send.at[block, slot],
            recv_sem=recv.at[block, slot],
            device_id={"zonal": device},
            device_id_type=pl.DeviceIdType.MESH,
        )

    def sides(block, half):
        return [
            pltpu.make_async_remote_copy(
                src_ref=pack.at[block, half],
                dst_ref=dst.at[block, half],
                send_sem=send.at[block, slot + 5 * half],
                recv_sem=recv.at[block, slot + 5 * half],
                device_id={"zonal": device},
                device_id_type=pl.DeviceIdType.MESH,
            )
            for slot, dst, device in ((0, west, right), (1, east, left))
        ]

    def fold(block, act):
        for slot, device, dst in ((3, a_east, feast), (4, a_west, fwest)):

            @pl.when(device != me)
            def _():
                act(copy(edge, dst, block, slot, device))

            @pl.when(device == me)
            def _():
                act(
                    pltpu.make_async_copy(
                        edge.at[block], dst.at[block], recv.at[block, slot]
                    )
                )

        act(copy(top, ftop, block, 2, across))

    def row(r):
        return pl.ds(r, channels, stride=pitch)

    def channel(c):
        return pl.ds(c * pitch, rows)

    def pack_top(block):
        acc = jnp.zeros((deep, width), F32)
        for k in range(3):
            cells = state[row(rows - 1 - k), :]
            top[block, k] = cells.astype(BF16)
            for part in range(channels // deep):
                at = (k * (channels // deep) + part) * FOLD
                inside = (lane_e >= at) & (lane_e < at + FOLD)
                acc = jnp.where(inside, roll(cells[part * deep : (part + 1) * deep], at + 3), acc)
        edge[block] = acc.astype(BF16)

    def pack_side(tile, each, size):
        at = lanes_of((size, width))
        acc = jnp.zeros((size, width), F32)
        for g in range(groups):
            inside = (at >= g * GROUP) & (at < (g + 1) * GROUP)
            acc = jnp.where(inside, roll(each(tile * groups + g), g * GROUP + 3), acc)
        return acc.astype(BF16)

    def send_half(block, half):
        for tile in range(tiles):
            pack[block, half, tile] = pack_side(
                tile, lambda c: state[pl.ds(c * pitch + half * deep, deep), :], deep
            )
        for each in sides(block, half):
            each.start()

    def columns(values):
        size = values.shape[1]
        return jnp.transpose(jnp.broadcast_to(values, (width, size)))

    def prepare(block):
        gains[block] = columns(gain_ref[block : block + 1])
        shifts[block] = columns(shift_ref[block : block + 1])
        bias = ba_ref[block : block + 1]
        high = bias.astype(BF16).astype(F32)
        extra = expand.shape[2] - channels
        at = rows_of((extra, hidden_units))
        tail = jnp.where(at == 0, high, jnp.where(at == 1, bias - high, 0.0)).astype(BF16)
        expand[block] = jnp.transpose(jnp.concatenate([wa_ref[block], tail], axis=0))
        contract[block] = wb_ref[block] * jnp.asarray(0.5, BF16)

    def bands(block):
        weights = jnp.transpose(dw_ref[:, block, :])
        tap = lax.broadcasted_iota(jnp.int32, (taps, 2 * width), 0)
        col = lax.broadcasted_iota(jnp.int32, (taps, 2 * width), 1)
        p, q = tap // 7, tap % 7
        hit = jnp.where(col // rows == q, col % rows + 3 - p, -1)
        narrow = weights.astype(BF16)
        for r in range(rows):
            pick = jnp.where(hit == r, 1.0, 0.0).astype(BF16)
            band = jnp.dot(narrow, pick, preferred_element_type=F32)
            t_low[block, row(r), :] = band[:, :width]
            t_high[block, row(r), :] = band[:, width:]

    def edge_weights(block):
        weights = dw_ref[:, block, :]
        spread = jnp.where(
            lanes_of((channels, tiles * width)) // GROUP == rows_of((channels, tiles * width)), 1.0, 0.0
        ).astype(BF16)
        wide = jnp.dot(weights.astype(BF16), spread, preferred_element_type=F32)
        slot = lanes_of((1, tiles * width)) % GROUP
        for p in range(7):
            for s in range(1, 4):
                low = jnp.where((slot < 3) & (slot + s >= 3), wide[7 * p + 3 + s : 7 * p + 4 + s], 0.0)
                high = jnp.where(
                    (slot >= 3) & (slot < 6) & (slot - s < 3), wide[7 * p + 3 - s : 7 * p + 4 - s], 0.0
                )
                side_w[block, 3 * p + s - 1 : 3 * p + s, :] = low + high
        turned = jnp.transpose(weights)
        for i in range(21):
            north_w[block, i] = jnp.broadcast_to(turned[:, 28 + i : 29 + i], (channels, width))

    def convolve(block):
        def parts(c):
            cells = state[channel(c), :]
            return jnp.concatenate(
                [(cells if j == 3 else roll(cells, 3 - j)).astype(BF16) for j in range(7)], axis=0
            )

        def band(c):
            at = channel(c)
            return jnp.concatenate([t_low[block, at, :], t_high[block, at, :]], axis=1).astype(BF16)[:, : 7 * rows]

        @pl.loop(0, channels // (2 * PAIRS))
        def _(index):
            for i in range(PAIRS):
                c = index * (2 * PAIRS) + 2 * i
                both = jnp.dot(
                    jnp.concatenate([band(c), band(c + 1)], axis=0),
                    jnp.concatenate([parts(c), parts(c + 1)], axis=1),
                    preferred_element_type=F32,
                )
                conv[channel(c), :] = both[:rows, :width]
                conv[channel(c + 1), :] = both[rows:, width:]

    def correct(block, half):
        first = deep - 3 if half else 0
        base = first // 8 * 8
        size = rows - base if half else deep
        slot = lane_e % GROUP
        at = rows_of((size, width)) + base
        column = lanes_of((size, width))
        outer = (column < 3) | (column >= width - 3)
        outer = outer & ((at >= first) if half else (at < deep - 3))
        for tile in range(tiles):
            diff = jnp.where(
                slot >= 3, east[block, half, tile].astype(F32), west[block, half, tile].astype(F32)
            ) - pack[block, half, tile].astype(F32)
            for s in range(1, 4):
                moved_ref[s - 1, tile, pl.ds(8 + half * deep, deep), :] = jnp.where(
                    slot < 3, roll(diff, -s), roll(diff, s)
                )
            total = jnp.zeros((size, width), F32)
            for p in range(7):
                for s in range(1, 4):
                    total = total + (
                        side_w[block, 3 * p + s - 1 : 3 * p + s, tile * width : (tile + 1) * width]
                        * moved_ref[s - 1, tile, pl.ds(base + 5 + p, size), :]
                    )
            for g in range(groups):
                here = pl.ds((tile * groups + g) * pitch + base, size)
                conv[here, :] += jnp.where(outer, roll(total, -(g * GROUP + 3)), 0.0)

    def add_north(block):
        flip = jnp.where(
            rows_of((width, width)) + lanes_of((width, width)) == width - 1, 1.0, 0.0
        ).astype(BF16)
        both = jnp.where(
            lane_e % FOLD >= 3, feast[block].astype(F32), fwest[block].astype(F32)
        )
        sums = [conv[row(rows - 3 + r), :] for r in range(3)]
        for k in range(3):
            parts = [
                roll(both, -((k * (channels // deep) + part) * FOLD + 3))
                for part in range(channels // deep)
            ]
            halo = jnp.dot(
                jnp.concatenate(parts, axis=0).astype(BF16), flip, preferred_element_type=F32
            )
            cells = jnp.dot(ftop[block, k], flip, preferred_element_type=F32)
            for q in range(7):
                moved = shifted(cells, halo, lane_c, q - 3)
                for r in range(k, 3):
                    sums[r] = sums[r] + north_w[block, 7 * (2 + k - r) + q] * moved
        for r in range(3):
            conv[row(rows - 3 + r), :] = sums[r]

    def mlp(block, start, step):
        extra = expand.shape[2] - channels
        ones = jnp.where(rows_of((extra, width)) < 2, 1.0, 0.0).astype(BF16)
        normed = []
        for k in range(step):
            y = conv[row(start + k), :]
            mean = jnp.sum(y, axis=0, keepdims=True) * (1.0 / channels)
            cent = y - mean
            var = jnp.sum(cent * cent, axis=0, keepdims=True) * (1.0 / channels)
            unit = (cent * lax.rsqrt(var + 1e-06) * gains[block] + shifts[block]).astype(BF16)
            normed.append(jnp.concatenate([unit, ones], axis=0))
        v = jnp.dot(
            expand[block], jnp.concatenate(normed, axis=1), preferred_element_type=F32
        ).astype(BF16)
        th = jnp.tanh(v * (jnp.asarray(K0, BF16) + jnp.asarray(K1, BF16) * (v * v)))
        outer = jnp.dot(contract[block], v + v * th, preferred_element_type=F32)
        for k in range(step):
            keep = mask_ref[pl.ds(start + k, 1), :].astype(F32)
            res = keep * (state[row(start + k), :] + outer[:, k * width : (k + 1) * width])
            state[row(start + k), :] = res.astype(BF16).astype(F32)

    moved_ref[...] = jnp.zeros(moved_ref.shape, F32)
    small[0].wait()
    maskf = mask_ref[...].astype(F32)
    for tile in range(tiles):
        load(tile).wait()

        def masked(c):
            cells = field_ref[c].astype(F32) * maskf
            state[channel(c), :] = cells
            return cells

        both = pack_side(tile, masked, rows)
        pack[0, 0, tile] = both[:deep]
        pack[0, 1, tile] = both[deep:]

    alone = jnp.where(a_east == me, 1, 0) + jnp.where(a_west == me, 1, 0)
    pl.semaphore_wait(barrier, 5 - alone)
    for half in range(2):
        for each in sides(0, half):
            each.start()
    pack_top(0)
    fold(0, lambda c: c.start())
    for each in small[1:]:
        each.wait()

    bands(0)
    convolve(0)
    for block in range(blocks):
        edge_weights(block)
        prepare(block)
        if block:
            bands(block)
    for block in range(blocks):
        if block:
            convolve(block)
        for each in sides(block, 0):
            each.wait()
        correct(block, 0)
        if block:
            mlp(block, 0, deep - 3)
        for each in sides(block, 1):
            each.wait()
        correct(block, 1)
        if block:
            mlp(block, deep - 3, rows - deep)
        else:
            mlp(block, 0, deep)
            if block < blocks - 1:
                send_half(block + 1, 0)
        fold(block, lambda c: c.wait())
        add_north(block)
        if block:
            mlp(block, rows - 3, 3)
        else:
            mlp(block, deep, rows - deep)
        if block < blocks - 1:
            if block:
                send_half(block + 1, 0)
            send_half(block + 1, 1)
            pack_top(block + 1)
            fold(block + 1, lambda c: c.start())


def finish(state, out_hbm, ready, sends):
    channels, rows, width = ready.shape
    pieces = sends.shape[0]
    size = channels // pieces
    copies = []
    for piece in range(pieces):
        for i in range(size):
            c = piece * size + i
            ready[c] = state[pl.ds(c * (rows + PAD), rows), :].astype(BF16)
        at = pl.ds(piece * size, size)
        copies.append(pltpu.make_async_copy(ready.at[at], out_hbm.at[at], sends.at[piece]))
        copies[-1].start()
    for each in copies:
        each.wait()


VMEM = pl.BlockSpec(memory_space=pltpu.VMEM)
HBM = pl.BlockSpec(memory_space=pltpu.HBM)


def local(field, land_mask, dw_weight, ln_gain, ln_shift, w_in, b_in, w_out):
    channels, rows, width = field.shape
    blocks = dw_weight.shape[0]
    tiles = channels * GROUP // width
    hidden = w_in.shape[1]
    flat = pltpu.VMEM((channels * (rows + PAD), width), F32)
    packed = pltpu.VMEM((blocks, 2, tiles, rows // 2, width), BF16)
    tops = pltpu.VMEM((blocks, 3, channels, width), BF16)
    edges = pltpu.VMEM((blocks, 16, width), BF16)
    wide = pltpu.VMEM((blocks, channels, width), F32)
    bands = pltpu.VMEM((blocks, channels * (rows + PAD), width), F32)
    args = (
        field,
        land_mask,
        jnp.swapaxes(dw_weight, 0, 1),
        ln_gain,
        ln_shift,
        jnp.swapaxes(w_in, 1, 2),
        b_in,
        w_out,
    )
    args = tuple(pltpu.with_memory_space_constraint(a, pltpu.HBM) for a in args)
    state = pl.pallas_call(
        functools.partial(kernel, lax.axis_size("zonal")),
        out_shape=flat,
        in_specs=[HBM] * 8,
        out_specs=VMEM,
        scratch_shapes=[pltpu.VMEM(a.shape, a.dtype) for a in args]
        + [
            flat,
            bands,
            bands,
            packed,
            tops,
            edges,
            packed,
            packed,
            tops,
            edges,
            edges,
            pltpu.VMEM((blocks, hidden, channels + 16), BF16),
            pltpu.VMEM((blocks, channels, hidden), BF16),
            wide,
            wide,
            pltpu.VMEM((3, tiles, rows + 16, width), F32),
            pltpu.VMEM((blocks, 24, tiles * width), F32),
            pltpu.VMEM((blocks, 21, channels, width), F32),
            pltpu.SemaphoreType.DMA((tiles + 7,)),
            pltpu.SemaphoreType.DMA((blocks, 7)),
            pltpu.SemaphoreType.DMA((blocks, 7)),
        ],
        compiler_params=pltpu.CompilerParams(
            collective_id=0, has_side_effects=True, vmem_limit_bytes=52 * 1024 * 1024
        ),
        name="evolve",
    )(*args)
    return pl.pallas_call(
        finish,
        out_shape=jax.ShapeDtypeStruct(field.shape, BF16),
        in_specs=[VMEM],
        out_specs=HBM,
        scratch_shapes=[
            pltpu.VMEM(field.shape, BF16),
            pltpu.SemaphoreType.DMA((tiles,)),
        ],
        compiler_params=pltpu.CompilerParams(vmem_limit_bytes=8 * 1024 * 1024),
        name="finish",
    )(state)


def solution(mesh):
    placed = (P("groups", None, "zonal"), P(None, "zonal"), P(), P(), P(), P(), P(), P())
    return jax.shard_map(
        local, mesh=mesh, in_specs=placed, out_specs=P("groups", None, "zonal"), check_vma=False
    )
```

```python
import functools

import jax
import jax.numpy as jnp
from jax import lax
from jax.experimental import pallas as pl
from jax.experimental.pallas import tpu as pltpu
from jax.sharding import PartitionSpec as P

F32 = jnp.float32
BF16 = jnp.bfloat16
GROUP = 8
FOLD = 6
PAD = 1
K0 = 0.7978845608028654
K1 = K0 * 0.044715


def roll(x, shift):
    return pltpu.roll(x, shift % x.shape[-1], axis=x.ndim - 1)


def lanes_of(shape):
    return lax.broadcasted_iota(jnp.int32, shape, len(shape) - 1)


def rows_of(shape):
    return lax.broadcasted_iota(jnp.int32, shape, len(shape) - 2)


def shifted(cells, halo, lane, d):
    width = cells.shape[-1]
    if d == 0:
        return cells
    beyond = lane < d if d > 0 else lane >= width + d
    return roll(jnp.where(beyond, halo, cells), -d)


def kernel(
    n, field_hbm, mask_hbm, dw_hbm, gain_hbm, shift_hbm, wa_hbm, ba_hbm, wb_hbm, state,
    field_ref, mask_ref, dw_ref, gain_ref, shift_ref, wa_ref, ba_ref, wb_ref,
    conv, t_low, t_high, pack, top, edge, west, east, ftop, feast, fwest, expand,
    contract, gains, shifts, keeps, fixes, side_w, north_w, loads, send, recv,
):
    channels, rows, width = field_ref.shape
    taps, blocks = dw_ref.shape[:2]
    hidden_units = wa_ref.shape[2]
    groups = width // GROUP
    tiles = channels // groups
    deep = edge.shape[1]
    span = width // deep
    calm = rows - 3
    pitch = rows + PAD
    outer_c = (lanes_of((channels, width)) < 3) | (lanes_of((channels, width)) >= width - 3)
    lane_c = lanes_of((channels, width))
    lane_e = lanes_of((deep, width))

    me = lax.axis_index("zonal")
    right, left = lax.rem(me + 1, n), lax.rem(me + n - 1, n)
    across = n - 1 - me
    a_east, a_west = lax.rem(across + 1, n), lax.rem(across + n - 1, n)
    barrier = pltpu.get_barrier_semaphore()

    def greet(device):
        pl.semaphore_signal(
            barrier, inc=1, device_id={"zonal": device}, device_id_type=pl.DeviceIdType.MESH
        )

    for device in (right, left, across):
        greet(device)

    @pl.when(a_east != me)
    def _():
        greet(a_east)

    @pl.when(a_west != me)
    def _():
        greet(a_west)

    def load(tile):
        at = pl.ds(tile * groups, groups)
        return pltpu.make_async_copy(field_hbm.at[at], field_ref.at[at], loads.at[tile])

    small = [
        pltpu.make_async_copy(src, dst, loads.at[tiles + i])
        for i, (src, dst) in enumerate(
            (
                (mask_hbm, mask_ref),
                (dw_hbm, dw_ref),
                (gain_hbm, gain_ref),
                (shift_hbm, shift_ref),
                (wa_hbm, wa_ref),
                (ba_hbm, ba_ref),
                (wb_hbm, wb_ref),
            )
        )
    ]
    small[0].start()
    for tile in range(tiles):
        load(tile).start()
    for each in small[1:]:
        each.start()

    def copy(src, dst, block, slot, device):
        return pltpu.make_async_remote_copy(
            src_ref=src.at[block],
            dst_ref=dst.at[block],
            send_sem=send.at[block, slot],
            recv_sem=recv.at[block, slot],
            device_id={"zonal": device},
            device_id_type=pl.DeviceIdType.MESH,
        )

    def sides(block, half):
        return [
            pltpu.make_async_remote_copy(
                src_ref=pack.at[block, half],
                dst_ref=dst.at[block, half],
                send_sem=send.at[block, slot + 5 * half],
                recv_sem=recv.at[block, slot + 5 * half],
                device_id={"zonal": device},
                device_id_type=pl.DeviceIdType.MESH,
            )
            for slot, dst, device in ((0, west, right), (1, east, left))
        ]

    def fold(block, act):
        for slot, device, dst in ((3, a_east, feast), (4, a_west, fwest)):

            @pl.when(device != me)
            def _():
                act(copy(edge, dst, block, slot, device))

            @pl.when(device == me)
            def _():
                act(
                    pltpu.make_async_copy(
                        edge.at[block], dst.at[block], recv.at[block, slot]
                    )
                )

        act(copy(top, ftop, block, 2, across))

    def row(r):
        return pl.ds(r, channels, stride=pitch)

    def channel(c):
        return pl.ds(c * pitch, rows)

    def pack_top(block):
        acc = jnp.zeros((deep, width), F32)
        for k in range(3):
            cells = state[row(rows - 1 - k), :]
            top[block, k] = cells.astype(BF16)
            for part in range(channels // deep):
                at = (k * (channels // deep) + part) * FOLD
                inside = (lane_e >= at) & (lane_e < at + FOLD)
                acc = jnp.where(inside, roll(cells[part * deep : (part + 1) * deep], at + 3), acc)
        edge[block] = acc.astype(BF16)

    def gather(total, r, values):
        at = lanes_of(values.shape)
        inside = (at >= r % deep * span) & (at < (r % deep + 1) * span)
        return jnp.where(inside, roll(values, r % deep * span + 3), total)

    def scatter(values, r):
        return roll(values, -(r % deep * span + 3))

    def send_half(block, half):
        for each in sides(block, half):
            each.start()

    def columns(values):
        size = values.shape[1]
        return jnp.transpose(jnp.broadcast_to(values, (width, size)))

    def prepare(block):
        gains[block] = columns(gain_ref[block : block + 1])
        shifts[block] = columns(shift_ref[block : block + 1])
        bias = ba_ref[block : block + 1]
        high = bias.astype(BF16).astype(F32)
        extra = expand.shape[2] - channels
        at = rows_of((extra, hidden_units))
        tail = jnp.where(at == 0, high, jnp.where(at == 1, bias - high, 0.0)).astype(BF16)
        expand[block] = jnp.transpose(jnp.concatenate([wa_ref[block], tail], axis=0))
        contract[block] = wb_ref[block] * jnp.asarray(0.5, BF16)

    def bands(block):
        weights = jnp.transpose(dw_ref[:, block, :])
        tap = lax.broadcasted_iota(jnp.int32, (taps, 2 * width), 0)
        col = lax.broadcasted_iota(jnp.int32, (taps, 2 * width), 1)
        p, q = tap // 7, tap % 7
        hit = jnp.where(col // rows == q, col % rows + 3 - p, -1)
        narrow = weights.astype(BF16)
        for r in range(rows):
            pick = jnp.where(hit == r, 1.0, 0.0).astype(BF16)
            band = jnp.dot(narrow, pick, preferred_element_type=F32)
            t_low[block, row(r), :] = band[:, :width]
            t_high[block, row(r), :] = band[:, width:]

    def edge_weights(block):
        weights = dw_ref[:, block, :]
        narrow = jnp.transpose(weights).astype(BF16)
        tap = rows_of((taps, width))
        slot = lanes_of((taps, width)) % span
        picks = []
        for p in range(7):
            for s in range(1, 4):
                low = (slot < 3) & (slot + s >= 3) & (tap == 7 * p + 3 + s)
                high = (slot >= 3) & (slot < 6) & (slot - s < 3) & (tap == 7 * p + 3 - s)
                picks.append(jnp.where(low | high, 1.0, 0.0).astype(BF16))
        wide = jnp.dot(narrow, jnp.concatenate(picks, axis=1), preferred_element_type=F32)
        for i in range(21):
            side_w[block, i] = wide[:, i * width : (i + 1) * width]
        turned = jnp.transpose(weights)
        for i in range(21):
            north_w[block, i] = jnp.broadcast_to(turned[:, 28 + i : 29 + i], (channels, width))

    def convolve(block):
        def parts(c):
            cells = state[channel(c), :]
            return jnp.concatenate(
                [(cells if j == 3 else roll(cells, 3 - j)).astype(BF16) for j in range(7)], axis=0
            )

        def band(c):
            at = channel(c)
            return jnp.concatenate([t_low[block, at, :], t_high[block, at, :]], axis=1).astype(BF16)[:, : 7 * rows]

        for c in range(0, channels, 2):
            both = jnp.dot(
                jnp.concatenate([band(c), band(c + 1)], axis=0),
                jnp.concatenate([parts(c), parts(c + 1)], axis=1),
                preferred_element_type=F32,
            )
            conv[channel(c), :] = both[:rows, :width]
            conv[channel(c + 1), :] = both[rows:, width:]

    def correct(block):
        slot = lane_c % span
        near = []
        for half in range(2):
            diff = jnp.where(
                slot >= 3, east[block, half].astype(F32), west[block, half].astype(F32)
            ) - pack[block, half].astype(F32)
            near.append([jnp.where(slot < 3, roll(diff, -s), roll(diff, s)) for s in range(1, 4)])
        total = [None, None]
        for p in (3, 0, 1, 2, 4, 5, 6):
            reach = span * abs(p - 3)
            moved = [
                roll(
                    side_w[block, 3 * p] * each[0]
                    + side_w[block, 3 * p + 1] * each[1]
                    + side_w[block, 3 * p + 2] * each[2],
                    span * (3 - p),
                )
                for each in near
            ]
            if p == 3:
                total = moved
            elif p < 3:
                total[0] = total[0] + jnp.where(lane_c >= reach, moved[0], 0.0)
                total[1] = total[1] + jnp.where(lane_c >= reach, moved[1], moved[0])
            else:
                total[0] = total[0] + jnp.where(lane_c < width - reach, moved[0], moved[1])
                total[1] = total[1] + jnp.where(lane_c < width - reach, moved[1], 0.0)
        return total

    def add_north(block, sums):
        flip = jnp.where(
            rows_of((width, width)) + lanes_of((width, width)) == width - 1, 1.0, 0.0
        ).astype(BF16)
        both = jnp.where(
            lane_e % FOLD >= 3, feast[block].astype(F32), fwest[block].astype(F32)
        )
        for k in range(3):
            parts = [
                roll(both, -((k * (channels // deep) + part) * FOLD + 3))
                for part in range(channels // deep)
            ]
            halo = jnp.dot(
                jnp.concatenate(parts, axis=0).astype(BF16), flip, preferred_element_type=F32
            )
            cells = jnp.dot(ftop[block, k], flip, preferred_element_type=F32)
            for q in range(7):
                moved = shifted(cells, halo, lane_c, q - 3)
                for r in range(k, 3):
                    sums[r] = sums[r] + north_w[block, 7 * (2 + k - r) + q] * moved
        return sums

    def net(block, values):
        extra = expand.shape[2] - channels
        ones = jnp.where(rows_of((extra, width)) < 2, 1.0, 0.0).astype(BF16)
        normed = []
        for y in values:
            mean = jnp.sum(y, axis=0, keepdims=True) * (1.0 / channels)
            cent = y - mean
            var = jnp.sum(cent * cent, axis=0, keepdims=True) * (1.0 / channels)
            unit = (cent * lax.rsqrt(var + 1e-06) * gains[block] + shifts[block]).astype(BF16)
            normed.append(jnp.concatenate([unit, ones], axis=0))
        v = jnp.dot(
            expand[block], jnp.concatenate(normed, axis=1), preferred_element_type=F32
        ).astype(BF16)
        th = jnp.tanh(v * (jnp.asarray(K0, BF16) + jnp.asarray(K1, BF16) * (v * v)))
        outer = jnp.dot(contract[block], v + v * th, preferred_element_type=F32)
        return [outer[:, k * width : (k + 1) * width] for k in range(len(values))]

    def keep(r):
        return mask_ref[pl.ds(r, 1), :].astype(F32)

    def inner(block, half):
        here = range(half * deep, min((half + 1) * deep, calm))
        values = [conv[row(r), :] for r in here]
        fix = jnp.zeros((channels, width), F32)
        for r, y in zip(here, values):
            fix = gather(fix, r, y)
        fixes[half] = fix
        for r, outer in zip(here, net(block, values)):
            res = keep(r) * (state[row(r), :] + outer)
            state[row(r), :] = res.astype(BF16).astype(F32)

    def border(block, total):
        outers = net(block, [fixes[half] + total[half] for half in range(2)])
        done = []
        for half in range(2):
            res = keeps[half : half + 1, :] * (pack[block, half].astype(F32) + outers[half])
            done.append(res.astype(BF16).astype(F32))
        return done

    def spread(done):
        for r in range(calm):
            state[row(r), :] = jnp.where(outer_c, scatter(done[r // deep], r), state[row(r), :])

    def crown(block, total):
        top_rows = range(calm, rows)
        values = [
            conv[row(r), :] + jnp.where(outer_c, scatter(total[1], r), 0.0) for r in top_rows
        ]
        results = []
        for r, outer in zip(top_rows, net(block, add_north(block, values))):
            res = (keep(r) * (state[row(r), :] + outer)).astype(BF16).astype(F32)
            state[row(r), :] = res
            results.append(res)
        return results

    small[0].wait()
    maskf = mask_ref[...].astype(F32)
    for tile in range(tiles):
        load(tile).wait()

        def masked(c):
            state[channel(c), :] = field_ref[c].astype(F32) * maskf

        for g in range(groups):
            masked(tile * groups + g)

    for half in range(2):
        total = jnp.zeros((channels, width), F32)
        for r in range(half * deep, (half + 1) * deep):
            total = gather(total, r, state[row(r), :])
        pack[0, half] = total.astype(BF16)
    alone = jnp.where(a_east == me, 1, 0) + jnp.where(a_west == me, 1, 0)
    pl.semaphore_wait(barrier, 5 - alone)
    for half in range(2):
        for each in sides(0, half):
            each.start()
    pack_top(0)
    fold(0, lambda c: c.start())
    for each in small[1:]:
        each.wait()

    bands(0)
    convolve(0)
    for half in range(2):
        total = jnp.zeros((8, width), F32)
        for r in range(half * deep, (half + 1) * deep):
            total = gather(total, r, jnp.broadcast_to(keep(r), total.shape))
        keeps[half : half + 1, :] = total[:1]
    for block in range(blocks):
        prepare(block)
        if block == 0:
            for half in range(2):
                inner(0, half)
        edge_weights(block)
        if block:
            bands(block)
    for block in range(blocks):
        more = block < blocks - 1
        if block:
            convolve(block)
            for half in range(2):
                inner(block, half)
        for half in range(2):
            for each in sides(block, half):
                each.wait()
        total = correct(block)
        done = border(block, total)
        if more:
            pack[block + 1, 0] = done[0].astype(BF16)
            send_half(block + 1, 0)
        spread(done)
        fold(block, lambda c: c.wait())
        results = crown(block, total)
        if more:
            rest = done[1]
            for r, res in zip(range(calm, rows), results):
                rest = gather(rest, r, res)
            pack[block + 1, 1] = rest.astype(BF16)
            send_half(block + 1, 1)
            pack_top(block + 1)
            fold(block + 1, lambda c: c.start())


def finish(state, out_hbm, ready, sends):
    channels, rows, width = ready.shape
    pieces = sends.shape[0]
    size = channels // pieces
    copies = []
    for piece in range(pieces):
        for i in range(size):
            c = piece * size + i
            ready[c] = state[pl.ds(c * (rows + PAD), rows), :].astype(BF16)
        at = pl.ds(piece * size, size)
        copies.append(pltpu.make_async_copy(ready.at[at], out_hbm.at[at], sends.at[piece]))
        copies[-1].start()
    for each in copies:
        each.wait()


VMEM = pl.BlockSpec(memory_space=pltpu.VMEM)
HBM = pl.BlockSpec(memory_space=pltpu.HBM)


def local(field, land_mask, dw_weight, ln_gain, ln_shift, w_in, b_in, w_out):
    channels, rows, width = field.shape
    blocks = dw_weight.shape[0]
    tiles = channels * GROUP // width
    hidden = w_in.shape[1]
    flat = pltpu.VMEM((channels * (rows + PAD), width), F32)
    packed = pltpu.VMEM((blocks, 2, channels, width), BF16)
    tops = pltpu.VMEM((blocks, 3, channels, width), BF16)
    edges = pltpu.VMEM((blocks, rows // 2, width), BF16)
    wide = pltpu.VMEM((blocks, channels, width), F32)
    bands = pltpu.VMEM((blocks, channels * (rows + PAD), width), F32)
    args = (
        field,
        land_mask,
        jnp.swapaxes(dw_weight, 0, 1),
        ln_gain,
        ln_shift,
        jnp.swapaxes(w_in, 1, 2),
        b_in,
        w_out,
    )
    args = tuple(pltpu.with_memory_space_constraint(a, pltpu.HBM) for a in args)
    state = pl.pallas_call(
        functools.partial(kernel, lax.axis_size("zonal")),
        out_shape=flat,
        in_specs=[HBM] * 8,
        out_specs=VMEM,
        scratch_shapes=[pltpu.VMEM(a.shape, a.dtype) for a in args]
        + [
            flat,
            bands,
            bands,
            packed,
            tops,
            edges,
            packed,
            packed,
            tops,
            edges,
            edges,
            pltpu.VMEM((blocks, hidden, channels + 16), BF16),
            pltpu.VMEM((blocks, channels, hidden), BF16),
            wide,
            wide,
            pltpu.VMEM((2, width), F32),
            pltpu.VMEM((2, channels, width), F32),
            pltpu.VMEM((blocks, 21, channels, width), F32),
            pltpu.VMEM((blocks, 21, channels, width), F32),
            pltpu.SemaphoreType.DMA((tiles + 7,)),
            pltpu.SemaphoreType.DMA((blocks, 7)),
            pltpu.SemaphoreType.DMA((blocks, 7)),
        ],
        compiler_params=pltpu.CompilerParams(
            collective_id=0, has_side_effects=True, vmem_limit_bytes=52 * 1024 * 1024
        ),
        name="evolve",
    )(*args)
    return pl.pallas_call(
        finish,
        out_shape=jax.ShapeDtypeStruct(field.shape, BF16),
        in_specs=[VMEM],
        out_specs=HBM,
        scratch_shapes=[
            pltpu.VMEM(field.shape, BF16),
            pltpu.SemaphoreType.DMA((tiles,)),
        ],
        compiler_params=pltpu.CompilerParams(vmem_limit_bytes=8 * 1024 * 1024),
        name="finish",
    )(state)


def solution(mesh):
    placed = (P("groups", None, "zonal"), P(None, "zonal"), P(), P(), P(), P(), P(), P())
    return jax.shard_map(
        local, mesh=mesh, in_specs=placed, out_specs=P("groups", None, "zonal"), check_vma=False
    )
```

```python
import functools

import jax
import jax.numpy as jnp
from jax import lax
from jax.experimental import pallas as pl
from jax.experimental.pallas import tpu as pltpu
from jax.sharding import PartitionSpec as P

F32 = jnp.float32
BF16 = jnp.bfloat16
GROUP = 8
FOLD = 6
PAD = 1
K0 = 0.7978845608028654
K1 = K0 * 0.044715


def roll(x, shift):
    return pltpu.roll(x, shift % x.shape[-1], axis=x.ndim - 1)


def lanes_of(shape):
    return lax.broadcasted_iota(jnp.int32, shape, len(shape) - 1)


def rows_of(shape):
    return lax.broadcasted_iota(jnp.int32, shape, len(shape) - 2)


def kernel(
    n, field_hbm, mask_hbm, dw_hbm, gain_hbm, shift_hbm, wa_hbm, ba_hbm, wb_hbm, state,
    field_ref, mask_ref, dw_ref, gain_ref, shift_ref, wa_ref, ba_ref, wb_ref,
    conv, t_low, t_high, pack, top, edge, west, east, ftop, feast, fwest, expand,
    contract, gains, shifts, keeps, fixes, side_w, north_w, turn, loads, send, recv,
):
    channels, rows, width = field_ref.shape
    taps, blocks = dw_ref.shape[:2]
    hidden_units = wa_ref.shape[2]
    groups = width // GROUP
    tiles = channels // groups
    deep = edge.shape[1]
    span = width // deep
    calm = rows - 3
    pitch = rows + PAD
    outer_c = (lanes_of((channels, width)) < 3) | (lanes_of((channels, width)) >= width - 3)
    lane_c = lanes_of((channels, width))
    lane_e = lanes_of((deep, width))

    me = lax.axis_index("zonal")
    right, left = lax.rem(me + 1, n), lax.rem(me + n - 1, n)
    across = n - 1 - me
    a_east, a_west = lax.rem(across + 1, n), lax.rem(across + n - 1, n)
    barrier = pltpu.get_barrier_semaphore()

    def greet(device):
        pl.semaphore_signal(
            barrier, inc=1, device_id={"zonal": device}, device_id_type=pl.DeviceIdType.MESH
        )

    for device in (right, left, across):
        greet(device)

    @pl.when(a_east != me)
    def _():
        greet(a_east)

    @pl.when(a_west != me)
    def _():
        greet(a_west)

    def load(tile):
        at = pl.ds(tile * groups, groups)
        return pltpu.make_async_copy(field_hbm.at[at], field_ref.at[at], loads.at[tile])

    small = [
        pltpu.make_async_copy(src, dst, loads.at[tiles + i])
        for i, (src, dst) in enumerate(
            (
                (mask_hbm, mask_ref),
                (dw_hbm, dw_ref),
                (gain_hbm, gain_ref),
                (shift_hbm, shift_ref),
                (wa_hbm, wa_ref),
                (ba_hbm, ba_ref),
                (wb_hbm, wb_ref),
            )
        )
    ]
    small[0].start()
    for tile in range(tiles):
        load(tile).start()
    for each in small[1:]:
        each.start()

    def copy(src, dst, block, slot, device):
        return pltpu.make_async_remote_copy(
            src_ref=src.at[block],
            dst_ref=dst.at[block],
            send_sem=send.at[block, slot],
            recv_sem=recv.at[block, slot],
            device_id={"zonal": device},
            device_id_type=pl.DeviceIdType.MESH,
        )

    def sides(block, half):
        return [
            pltpu.make_async_remote_copy(
                src_ref=pack.at[block, half],
                dst_ref=dst.at[block, half],
                send_sem=send.at[block, slot + 5 * half],
                recv_sem=recv.at[block, slot + 5 * half],
                device_id={"zonal": device},
                device_id_type=pl.DeviceIdType.MESH,
            )
            for slot, dst, device in ((0, west, right), (1, east, left))
        ]

    def fold(block, act):
        for slot, device, dst in ((3, a_east, feast), (4, a_west, fwest)):

            @pl.when(device != me)
            def _():
                act(copy(edge, dst, block, slot, device))

            @pl.when(device == me)
            def _():
                act(
                    pltpu.make_async_copy(
                        edge.at[block], dst.at[block], recv.at[block, slot]
                    )
                )

        act(copy(top, ftop, block, 2, across))

    def row(r):
        return pl.ds(r, channels, stride=pitch)

    def channel(c):
        return pl.ds(c * pitch, rows)

    def pack_top(block):
        acc = jnp.zeros((deep, width), F32)
        for k in range(3):
            cells = state[row(rows - 1 - k), :]
            top[block, k] = cells.astype(BF16)
            for part in range(channels // deep):
                at = (k * (channels // deep) + part) * FOLD
                inside = (lane_e >= at) & (lane_e < at + FOLD)
                acc = jnp.where(inside, roll(cells[part * deep : (part + 1) * deep], at + 3), acc)
        edge[block] = acc.astype(BF16)

    def gather(total, r, values):
        at = lanes_of(values.shape)
        inside = (at >= r % deep * span) & (at < (r % deep + 1) * span)
        return jnp.where(inside, roll(values, r % deep * span + 3), total)

    def scatter(values, r):
        return roll(values, -(r % deep * span + 3))

    def send_half(block, half):
        for each in sides(block, half):
            each.start()

    def columns(values):
        size = values.shape[1]
        return jnp.transpose(jnp.broadcast_to(values, (width, size)))

    def prepare(block):
        gains[block] = columns(gain_ref[block : block + 1])
        shifts[block] = columns(shift_ref[block : block + 1])
        bias = ba_ref[block : block + 1]
        high = bias.astype(BF16).astype(F32)
        extra = expand.shape[2] - channels
        at = rows_of((extra, hidden_units))
        tail = jnp.where(at == 0, high, jnp.where(at == 1, bias - high, 0.0)).astype(BF16)
        expand[block] = jnp.transpose(jnp.concatenate([wa_ref[block], tail], axis=0))
        contract[block] = wb_ref[block] * jnp.asarray(0.5, BF16)

    def bands(block):
        weights = jnp.transpose(dw_ref[:, block, :])
        tap = lax.broadcasted_iota(jnp.int32, (taps, 2 * width), 0)
        col = lax.broadcasted_iota(jnp.int32, (taps, 2 * width), 1)
        p, q = tap // 7, tap % 7
        hit = jnp.where(col // rows == q, col % rows + 3 - p, -1)
        narrow = weights.astype(BF16)
        for r in range(rows):
            pick = jnp.where(hit == r, 1.0, 0.0).astype(BF16)
            band = jnp.dot(narrow, pick, preferred_element_type=F32)
            t_low[block, row(r), :] = band[:, :width]
            t_high[block, row(r), :] = band[:, width:]

    def edge_weights(block):
        weights = dw_ref[:, block, :]
        narrow = jnp.transpose(weights).astype(BF16)
        tap = rows_of((taps, width))
        slot = lanes_of((taps, width)) % span
        picks = []
        for p in range(7):
            for s in range(1, 4):
                low = (slot < 3) & (slot + s >= 3) & (tap == 7 * p + 3 + s)
                high = (slot >= 3) & (slot < 6) & (slot - s < 3) & (tap == 7 * p + 3 - s)
                picks.append(jnp.where(low | high, 1.0, 0.0).astype(BF16))
        wide = jnp.dot(narrow, jnp.concatenate(picks, axis=1), preferred_element_type=F32)
        for i in range(21):
            side_w[block, i] = wide[:, i * width : (i + 1) * width]
        turned = jnp.transpose(weights)
        for i in range(21):
            north_w[block, i] = jnp.broadcast_to(turned[:, 28 + i : 29 + i], (channels, width))

    def convolve(block):
        def parts(c):
            cells = state[channel(c), :]
            return jnp.concatenate(
                [(cells if j == 3 else roll(cells, 3 - j)).astype(BF16) for j in range(7)], axis=0
            )

        def band(c):
            at = channel(c)
            return jnp.concatenate([t_low[block, at, :], t_high[block, at, :]], axis=1).astype(BF16)[:, : 7 * rows]

        for c in range(0, channels, 2):
            both = jnp.dot(
                jnp.concatenate([band(c), band(c + 1)], axis=0),
                jnp.concatenate([parts(c), parts(c + 1)], axis=1),
                preferred_element_type=F32,
            )
            conv[channel(c), :] = both[:rows, :width]
            conv[channel(c + 1), :] = both[rows:, width:]

    def correct(block):
        slot = lane_c % span
        near = []
        for half in range(2):
            diff = jnp.where(
                slot >= 3, east[block, half].astype(F32), west[block, half].astype(F32)
            ) - pack[block, half].astype(F32)
            near.append([jnp.where(slot < 3, roll(diff, -s), roll(diff, s)) for s in range(1, 4)])
        total = [None, None]
        for p in (3, 0, 1, 2, 4, 5, 6):
            reach = span * abs(p - 3)
            moved = [
                roll(
                    side_w[block, 3 * p] * each[0]
                    + side_w[block, 3 * p + 1] * each[1]
                    + side_w[block, 3 * p + 2] * each[2],
                    span * (3 - p),
                )
                for each in near
            ]
            if p == 3:
                total = moved
            elif p < 3:
                total[0] = total[0] + jnp.where(lane_c >= reach, moved[0], 0.0)
                total[1] = total[1] + jnp.where(lane_c >= reach, moved[1], moved[0])
            else:
                total[0] = total[0] + jnp.where(lane_c < width - reach, moved[0], moved[1])
                total[1] = total[1] + jnp.where(lane_c < width - reach, moved[1], 0.0)
        return total

    def turns():
        source = rows_of((width, width))
        target = lanes_of((width, width))
        for q in range(7):
            at = target + (q - 3)
            back = width - 1 - at
            inside = (at >= 0) & (at < width)
            here = pl.ds(q * width, width)
            turn[:width, here] = jnp.where(inside & (source == back), 1.0, 0.0).astype(BF16)
            turn[width:, here] = jnp.where(
                jnp.logical_not(inside) & ((source == back + width) | (source == back - width)),
                1.0,
                0.0,
            ).astype(BF16)

    def add_north(block, sums):
        both = jnp.where(
            lane_e % FOLD >= 3, feast[block].astype(F32), fwest[block].astype(F32)
        )
        for k in range(3):
            parts = [
                roll(both, -((k * (channels // deep) + part) * FOLD + 3))
                for part in range(channels // deep)
            ]
            halo = jnp.concatenate(parts, axis=0).astype(BF16)
            moved = jnp.dot(
                jnp.concatenate([ftop[block, k], halo], axis=1),
                turn[...],
                preferred_element_type=F32,
            )
            for q in range(7):
                for r in range(k, 3):
                    sums[r] = sums[r] + (
                        north_w[block, 7 * (2 + k - r) + q] * moved[:, q * width : (q + 1) * width]
                    )
        return sums

    def net(block, values):
        extra = expand.shape[2] - channels
        ones = jnp.where(rows_of((extra, width)) < 2, 1.0, 0.0).astype(BF16)
        normed = []
        for y in values:
            mean = jnp.sum(y, axis=0, keepdims=True) * (1.0 / channels)
            cent = y - mean
            var = jnp.sum(cent * cent, axis=0, keepdims=True) * (1.0 / channels)
            unit = (cent * lax.rsqrt(var + 1e-06) * gains[block] + shifts[block]).astype(BF16)
            normed.append(jnp.concatenate([unit, ones], axis=0))
        v = jnp.dot(
            expand[block], jnp.concatenate(normed, axis=1), preferred_element_type=F32
        ).astype(BF16)
        th = jnp.tanh(v * (jnp.asarray(K0, BF16) + jnp.asarray(K1, BF16) * (v * v)))
        outer = jnp.dot(contract[block], v + v * th, preferred_element_type=F32)
        return [outer[:, k * width : (k + 1) * width] for k in range(len(values))]

    def keep(r):
        return mask_ref[pl.ds(r, 1), :].astype(F32)

    def inner(block, half):
        here = range(half * deep, min((half + 1) * deep, calm))
        values = [conv[row(r), :] for r in here]
        fix = jnp.zeros((channels, width), F32)
        for r, y in zip(here, values):
            fix = gather(fix, r, y)
        fixes[half] = fix
        for r, outer in zip(here, net(block, values)):
            res = keep(r) * (state[row(r), :] + outer)
            state[row(r), :] = res.astype(BF16).astype(F32)

    def border(block, total):
        outers = net(block, [fixes[half] + total[half] for half in range(2)])
        done = []
        for half in range(2):
            res = keeps[half : half + 1, :] * (pack[block, half].astype(F32) + outers[half])
            done.append(res.astype(BF16).astype(F32))
        return done

    def spread(done):
        for r in range(calm):
            state[row(r), :] = jnp.where(outer_c, scatter(done[r // deep], r), state[row(r), :])

    def crown(block, total):
        top_rows = range(calm, rows)
        values = [
            conv[row(r), :] + jnp.where(outer_c, scatter(total[1], r), 0.0) for r in top_rows
        ]
        results = []
        for r, outer in zip(top_rows, net(block, add_north(block, values))):
            res = (keep(r) * (state[row(r), :] + outer)).astype(BF16).astype(F32)
            state[row(r), :] = res
            results.append(res)
        return results

    small[0].wait()
    maskf = mask_ref[...].astype(F32)
    for tile in range(tiles):
        load(tile).wait()

        def masked(c):
            state[channel(c), :] = field_ref[c].astype(F32) * maskf

        for g in range(groups):
            masked(tile * groups + g)

    for half in range(2):
        total = jnp.zeros((channels, width), F32)
        for r in range(half * deep, (half + 1) * deep):
            total = gather(total, r, state[row(r), :])
        pack[0, half] = total.astype(BF16)
    alone = jnp.where(a_east == me, 1, 0) + jnp.where(a_west == me, 1, 0)
    pl.semaphore_wait(barrier, 5 - alone)
    for half in range(2):
        for each in sides(0, half):
            each.start()
    pack_top(0)
    fold(0, lambda c: c.start())
    for each in small[1:]:
        each.wait()

    bands(0)
    convolve(0)
    for half in range(2):
        total = jnp.zeros((8, width), F32)
        for r in range(half * deep, (half + 1) * deep):
            total = gather(total, r, jnp.broadcast_to(keep(r), total.shape))
        keeps[half : half + 1, :] = total[:1]
    prepare(0)
    for half in range(2):
        inner(0, half)
    turns()
    edge_weights(0)
    for block in range(blocks):
        more = block < blocks - 1
        if block:
            bands(block)
            convolve(block)
            prepare(block)
            for half in range(2):
                inner(block, half)
            edge_weights(block)
        for half in range(2):
            for each in sides(block, half):
                each.wait()
        total = correct(block)
        done = border(block, total)
        if more:
            pack[block + 1, 0] = done[0].astype(BF16)
            send_half(block + 1, 0)
        spread(done)
        fold(block, lambda c: c.wait())
        results = crown(block, total)
        if more:
            rest = done[1]
            for r, res in zip(range(calm, rows), results):
                rest = gather(rest, r, res)
            pack[block + 1, 1] = rest.astype(BF16)
            send_half(block + 1, 1)
            pack_top(block + 1)
            fold(block + 1, lambda c: c.start())


def finish(state, out_hbm, ready, sends):
    channels, rows, width = ready.shape
    pieces = sends.shape[0]
    size = channels // pieces
    copies = []
    for piece in range(pieces):
        for i in range(size):
            c = piece * size + i
            ready[c] = state[pl.ds(c * (rows + PAD), rows), :].astype(BF16)
        at = pl.ds(piece * size, size)
        copies.append(pltpu.make_async_copy(ready.at[at], out_hbm.at[at], sends.at[piece]))
        copies[-1].start()
    for each in copies:
        each.wait()


VMEM = pl.BlockSpec(memory_space=pltpu.VMEM)
HBM = pl.BlockSpec(memory_space=pltpu.HBM)


def local(field, land_mask, dw_weight, ln_gain, ln_shift, w_in, b_in, w_out):
    channels, rows, width = field.shape
    blocks = dw_weight.shape[0]
    tiles = channels * GROUP // width
    hidden = w_in.shape[1]
    flat = pltpu.VMEM((channels * (rows + PAD), width), F32)
    packed = pltpu.VMEM((blocks, 2, channels, width), BF16)
    tops = pltpu.VMEM((blocks, 3, channels, width), BF16)
    edges = pltpu.VMEM((blocks, rows // 2, width), BF16)
    wide = pltpu.VMEM((blocks, channels, width), F32)
    bands = pltpu.VMEM((blocks, channels * (rows + PAD), width), F32)
    args = (
        field,
        land_mask,
        jnp.swapaxes(dw_weight, 0, 1),
        ln_gain,
        ln_shift,
        jnp.swapaxes(w_in, 1, 2),
        b_in,
        w_out,
    )
    args = tuple(pltpu.with_memory_space_constraint(a, pltpu.HBM) for a in args)
    state = pl.pallas_call(
        functools.partial(kernel, lax.axis_size("zonal")),
        out_shape=flat,
        in_specs=[HBM] * 8,
        out_specs=VMEM,
        scratch_shapes=[pltpu.VMEM(a.shape, a.dtype) for a in args]
        + [
            flat,
            bands,
            bands,
            packed,
            tops,
            edges,
            packed,
            packed,
            tops,
            edges,
            edges,
            pltpu.VMEM((blocks, hidden, channels + 16), BF16),
            pltpu.VMEM((blocks, channels, hidden), BF16),
            wide,
            wide,
            pltpu.VMEM((2, width), F32),
            pltpu.VMEM((2, channels, width), F32),
            pltpu.VMEM((blocks, 21, channels, width), F32),
            pltpu.VMEM((blocks, 21, channels, width), F32),
            pltpu.VMEM((2 * width, 7 * width), BF16),
            pltpu.SemaphoreType.DMA((tiles + 7,)),
            pltpu.SemaphoreType.DMA((blocks, 7)),
            pltpu.SemaphoreType.DMA((blocks, 7)),
        ],
        compiler_params=pltpu.CompilerParams(
            collective_id=0, has_side_effects=True, vmem_limit_bytes=52 * 1024 * 1024
        ),
        name="evolve",
    )(*args)
    return pl.pallas_call(
        finish,
        out_shape=jax.ShapeDtypeStruct(field.shape, BF16),
        in_specs=[VMEM],
        out_specs=HBM,
        scratch_shapes=[
            pltpu.VMEM(field.shape, BF16),
            pltpu.SemaphoreType.DMA((tiles,)),
        ],
        compiler_params=pltpu.CompilerParams(vmem_limit_bytes=8 * 1024 * 1024),
        name="finish",
    )(state)


def solution(mesh):
    placed = (P("groups", None, "zonal"), P(None, "zonal"), P(), P(), P(), P(), P(), P())
    return jax.shard_map(
        local, mesh=mesh, in_specs=placed, out_specs=P("groups", None, "zonal"), check_vma=False
    )
```

```python
import functools

import jax
import jax.numpy as jnp
from jax import lax
from jax.experimental import pallas as pl
from jax.experimental.pallas import tpu as pltpu
from jax.sharding import PartitionSpec as P

F32 = jnp.float32
BF16 = jnp.bfloat16
GROUP = 8
FOLD = 6
PAD = 1
K0 = 0.7978845608028654
K1 = K0 * 0.044715


def roll(x, shift):
    return pltpu.roll(x, shift % x.shape[-1], axis=x.ndim - 1)


def lanes_of(shape):
    return lax.broadcasted_iota(jnp.int32, shape, len(shape) - 1)


def rows_of(shape):
    return lax.broadcasted_iota(jnp.int32, shape, len(shape) - 2)


def kernel(
    n, field_hbm, mask_hbm, dw_hbm, gain_hbm, shift_hbm, wa_hbm, ba_hbm, wb_hbm, state,
    field_ref, mask_ref, dw_ref, gain_ref, shift_ref, wa_ref, ba_ref, wb_ref,
    conv, t_low, t_high, pack, top, edge, west, east, ftop, feast, fwest, expand,
    contract, gains, shifts, keeps, fixes, side_w, north_w, turn, loads, send, recv,
):
    channels, rows, width = field_ref.shape
    taps, blocks = dw_ref.shape[:2]
    hidden_units = wa_ref.shape[2]
    groups = width // GROUP
    tiles = channels // groups
    deep = edge.shape[1]
    span = width // deep
    calm = rows - 3
    pitch = rows + PAD
    outer_c = (lanes_of((channels, width)) < 3) | (lanes_of((channels, width)) >= width - 3)
    lane_c = lanes_of((channels, width))
    lane_e = lanes_of((deep, width))

    me = lax.axis_index("zonal")
    right, left = lax.rem(me + 1, n), lax.rem(me + n - 1, n)
    across = n - 1 - me
    a_east, a_west = lax.rem(across + 1, n), lax.rem(across + n - 1, n)
    barrier = pltpu.get_barrier_semaphore()

    def greet(device):
        pl.semaphore_signal(
            barrier, inc=1, device_id={"zonal": device}, device_id_type=pl.DeviceIdType.MESH
        )

    for device in (right, left, across):
        greet(device)

    @pl.when(a_east != me)
    def _():
        greet(a_east)

    @pl.when(a_west != me)
    def _():
        greet(a_west)

    def load(tile):
        at = pl.ds(tile * groups, groups)
        return pltpu.make_async_copy(field_hbm.at[at], field_ref.at[at], loads.at[tile])

    small = [
        pltpu.make_async_copy(src, dst, loads.at[tiles + i])
        for i, (src, dst) in enumerate(
            (
                (mask_hbm, mask_ref),
                (dw_hbm, dw_ref),
                (gain_hbm, gain_ref),
                (shift_hbm, shift_ref),
                (wa_hbm, wa_ref),
                (ba_hbm, ba_ref),
                (wb_hbm, wb_ref),
            )
        )
    ]
    small[0].start()
    for tile in range(tiles):
        load(tile).start()
    for each in small[1:]:
        each.start()

    def copy(src, dst, block, slot, device):
        return pltpu.make_async_remote_copy(
            src_ref=src.at[block],
            dst_ref=dst.at[block],
            send_sem=send.at[block, slot],
            recv_sem=recv.at[block, slot],
            device_id={"zonal": device},
            device_id_type=pl.DeviceIdType.MESH,
        )

    def sides(block, half):
        return [
            pltpu.make_async_remote_copy(
                src_ref=pack.at[block, half] if block else pack.at[block],
                dst_ref=dst.at[block, half] if block else dst.at[block],
                send_sem=send.at[block, slot + 5 * half],
                recv_sem=recv.at[block, slot + 5 * half],
                device_id={"zonal": device},
                device_id_type=pl.DeviceIdType.MESH,
            )
            for slot, dst, device in ((0, west, right), (1, east, left))
        ]

    def fold(block, act):
        for slot, device, dst in ((3, a_east, feast), (4, a_west, fwest)):

            @pl.when(device != me)
            def _():
                act(copy(edge, dst, block, slot, device))

            @pl.when(device == me)
            def _():
                act(
                    pltpu.make_async_copy(
                        edge.at[block], dst.at[block], recv.at[block, slot]
                    )
                )

        act(copy(top, ftop, block, 2, across))

    def row(r):
        return pl.ds(r, channels, stride=pitch)

    def channel(c):
        return pl.ds(c * pitch, rows)

    def pack_top(block):
        acc = jnp.zeros((deep, width), F32)
        for k in range(3):
            cells = state[row(rows - 1 - k), :]
            top[block, k] = cells.astype(BF16)
            for part in range(channels // deep):
                at = (k * (channels // deep) + part) * FOLD
                inside = (lane_e >= at) & (lane_e < at + FOLD)
                acc = jnp.where(inside, roll(cells[part * deep : (part + 1) * deep], at + 3), acc)
        edge[block] = acc.astype(BF16)

    def gather(total, r, values):
        at = lanes_of(values.shape)
        inside = (at >= r % deep * span) & (at < (r % deep + 1) * span)
        return jnp.where(inside, roll(values, r % deep * span + 3), total)

    def scatter(values, r):
        return roll(values, -(r % deep * span + 3))

    def send_half(block, half):
        for each in sides(block, half):
            each.start()

    def columns(values):
        size = values.shape[1]
        return jnp.transpose(jnp.broadcast_to(values, (width, size)))

    def prepare(block):
        gains[block] = columns(gain_ref[block : block + 1])
        shifts[block] = columns(shift_ref[block : block + 1])
        bias = ba_ref[block : block + 1]
        high = bias.astype(BF16).astype(F32)
        extra = expand.shape[2] - channels
        at = rows_of((extra, hidden_units))
        tail = jnp.where(at == 0, high, jnp.where(at == 1, bias - high, 0.0)).astype(BF16)
        expand[block] = jnp.transpose(jnp.concatenate([wa_ref[block], tail], axis=0))
        contract[block] = wb_ref[block] * jnp.asarray(0.5, BF16)

    def bands(block):
        weights = jnp.transpose(dw_ref[:, block, :])
        tap = lax.broadcasted_iota(jnp.int32, (taps, 2 * width), 0)
        col = lax.broadcasted_iota(jnp.int32, (taps, 2 * width), 1)
        p, q = tap // 7, tap % 7
        hit = jnp.where(col // rows == q, col % rows + 3 - p, -1)
        narrow = weights.astype(BF16)
        for r in range(rows):
            pick = jnp.where(hit == r, 1.0, 0.0).astype(BF16)
            band = jnp.dot(narrow, pick, preferred_element_type=F32)
            t_low[block, row(r), :] = band[:, :width]
            t_high[block, row(r), :] = band[:, width:]

    def edge_weights(block):
        weights = dw_ref[:, block, :]
        narrow = jnp.transpose(weights).astype(BF16)
        tap = rows_of((taps, width))
        slot = lanes_of((taps, width)) % span
        picks = []
        for p in range(7):
            for s in range(1, 4):
                low = (slot < 3) & (slot + s >= 3) & (tap == 7 * p + 3 + s)
                high = (slot >= 3) & (slot < 6) & (slot - s < 3) & (tap == 7 * p + 3 - s)
                picks.append(jnp.where(low | high, 1.0, 0.0).astype(BF16))
        wide = jnp.dot(narrow, jnp.concatenate(picks, axis=1), preferred_element_type=F32)
        for i in range(21):
            side_w[block, i] = wide[:, i * width : (i + 1) * width]
        turned = jnp.transpose(weights)
        for i in range(21):
            north_w[block, i] = jnp.broadcast_to(turned[:, 28 + i : 29 + i], (channels, width))

    def convolve(block):
        def parts(c):
            cells = state[channel(c), :]
            return jnp.concatenate(
                [(cells if j == 3 else roll(cells, 3 - j)).astype(BF16) for j in range(7)], axis=0
            )

        def band(c):
            at = channel(c)
            return jnp.concatenate([t_low[block, at, :], t_high[block, at, :]], axis=1).astype(BF16)[:, : 7 * rows]

        for c in range(0, channels, 2):
            both = jnp.dot(
                jnp.concatenate([band(c), band(c + 1)], axis=0),
                jnp.concatenate([parts(c), parts(c + 1)], axis=1),
                preferred_element_type=F32,
            )
            conv[channel(c), :] = both[:rows, :width]
            conv[channel(c + 1), :] = both[rows:, width:]

    def correct(block):
        slot = lane_c % span
        near = []
        for half in range(2):
            diff = jnp.where(
                slot >= 3, east[block, half].astype(F32), west[block, half].astype(F32)
            ) - pack[block, half].astype(F32)
            near.append([jnp.where(slot < 3, roll(diff, -s), roll(diff, s)) for s in range(1, 4)])
        total = [None, None]
        for p in (3, 0, 1, 2, 4, 5, 6):
            reach = span * abs(p - 3)
            moved = [
                roll(
                    side_w[block, 3 * p] * each[0]
                    + side_w[block, 3 * p + 1] * each[1]
                    + side_w[block, 3 * p + 2] * each[2],
                    span * (3 - p),
                )
                for each in near
            ]
            if p == 3:
                total = moved
            elif p < 3:
                total[0] = total[0] + jnp.where(lane_c >= reach, moved[0], 0.0)
                total[1] = total[1] + jnp.where(lane_c >= reach, moved[1], moved[0])
            else:
                total[0] = total[0] + jnp.where(lane_c < width - reach, moved[0], moved[1])
                total[1] = total[1] + jnp.where(lane_c < width - reach, moved[1], 0.0)
        return total

    def turns():
        source = rows_of((width, width))
        target = lanes_of((width, width))
        for q in range(7):
            at = target + (q - 3)
            back = width - 1 - at
            inside = (at >= 0) & (at < width)
            here = pl.ds(q * width, width)
            turn[:width, here] = jnp.where(inside & (source == back), 1.0, 0.0).astype(BF16)
            turn[width:, here] = jnp.where(
                jnp.logical_not(inside) & ((source == back + width) | (source == back - width)),
                1.0,
                0.0,
            ).astype(BF16)

    def add_north(block, sums):
        both = jnp.where(
            lane_e % FOLD >= 3, feast[block].astype(F32), fwest[block].astype(F32)
        )
        for k in range(3):
            parts = [
                roll(both, -((k * (channels // deep) + part) * FOLD + 3))
                for part in range(channels // deep)
            ]
            halo = jnp.concatenate(parts, axis=0).astype(BF16)
            moved = jnp.dot(
                jnp.concatenate([ftop[block, k], halo], axis=1),
                turn[...],
                preferred_element_type=F32,
            )
            for q in range(7):
                for r in range(k, 3):
                    sums[r] = sums[r] + (
                        north_w[block, 7 * (2 + k - r) + q] * moved[:, q * width : (q + 1) * width]
                    )
        return sums

    def net(block, values):
        extra = expand.shape[2] - channels
        ones = jnp.where(rows_of((extra, width)) < 2, 1.0, 0.0).astype(BF16)
        normed = []
        for y in values:
            mean = jnp.sum(y, axis=0, keepdims=True) * (1.0 / channels)
            cent = y - mean
            var = jnp.sum(cent * cent, axis=0, keepdims=True) * (1.0 / channels)
            unit = (cent * lax.rsqrt(var + 1e-06) * gains[block] + shifts[block]).astype(BF16)
            normed.append(jnp.concatenate([unit, ones], axis=0))
        v = jnp.dot(
            expand[block], jnp.concatenate(normed, axis=1), preferred_element_type=F32
        ).astype(BF16)
        th = jnp.tanh(v * (jnp.asarray(K0, BF16) + jnp.asarray(K1, BF16) * (v * v)))
        outer = jnp.dot(contract[block], v + v * th, preferred_element_type=F32)
        return [outer[:, k * width : (k + 1) * width] for k in range(len(values))]

    def keep(r):
        return mask_ref[pl.ds(r, 1), :].astype(F32)

    def inner(block, half):
        here = range(half * deep, min((half + 1) * deep, calm))
        values = [conv[row(r), :] for r in here]
        fix = jnp.zeros((channels, width), F32)
        for r, y in zip(here, values):
            fix = gather(fix, r, y)
        fixes[half] = fix
        for r, outer in zip(here, net(block, values)):
            res = keep(r) * (state[row(r), :] + outer)
            state[row(r), :] = res.astype(BF16).astype(F32)

    def border(block, total):
        outers = net(block, [fixes[half] + total[half] for half in range(2)])
        done = []
        for half in range(2):
            res = keeps[half : half + 1, :] * (pack[block, half].astype(F32) + outers[half])
            done.append(res.astype(BF16).astype(F32))
        return done

    def spread(done):
        for r in range(calm):
            state[row(r), :] = jnp.where(outer_c, scatter(done[r // deep], r), state[row(r), :])

    def crown(block, total):
        top_rows = range(calm, rows)
        values = [
            conv[row(r), :] + jnp.where(outer_c, scatter(total[1], r), 0.0) for r in top_rows
        ]
        results = []
        for r, outer in zip(top_rows, net(block, add_north(block, values))):
            res = (keep(r) * (state[row(r), :] + outer)).astype(BF16).astype(F32)
            state[row(r), :] = res
            results.append(res)
        return results

    small[0].wait()
    maskf = mask_ref[...].astype(F32)
    for tile in range(tiles):
        load(tile).wait()

        def masked(c):
            state[channel(c), :] = field_ref[c].astype(F32) * maskf

        for g in range(groups):
            masked(tile * groups + g)

    for half in range(2):
        total = jnp.zeros((channels, width), F32)
        for r in range(half * deep, (half + 1) * deep):
            total = gather(total, r, state[row(r), :])
        pack[0, half] = total.astype(BF16)
    alone = jnp.where(a_east == me, 1, 0) + jnp.where(a_west == me, 1, 0)
    pl.semaphore_wait(barrier, 5 - alone)
    for each in sides(0, 0):
        each.start()
    pack_top(0)
    fold(0, lambda c: c.start())
    for each in small[1:]:
        each.wait()

    bands(0)
    convolve(0)
    for half in range(2):
        total = jnp.zeros((8, width), F32)
        for r in range(half * deep, (half + 1) * deep):
            total = gather(total, r, jnp.broadcast_to(keep(r), total.shape))
        keeps[half : half + 1, :] = total[:1]
    prepare(0)
    for half in range(2):
        inner(0, half)
    turns()
    edge_weights(0)
    for block in range(blocks):
        more = block < blocks - 1
        if block:
            bands(block)
            convolve(block)
            prepare(block)
            for half in range(2):
                inner(block, half)
            edge_weights(block)
        for half in range(2 if block else 1):
            for each in sides(block, half):
                each.wait()
        total = correct(block)
        done = border(block, total)
        if more:
            pack[block + 1, 0] = done[0].astype(BF16)
            send_half(block + 1, 0)
        spread(done)
        fold(block, lambda c: c.wait())
        results = crown(block, total)
        if more:
            rest = done[1]
            for r, res in zip(range(calm, rows), results):
                rest = gather(rest, r, res)
            pack[block + 1, 1] = rest.astype(BF16)
            send_half(block + 1, 1)
            pack_top(block + 1)
            fold(block + 1, lambda c: c.start())


def finish(state, out_hbm, ready, sends):
    channels, rows, width = ready.shape
    pieces = sends.shape[0]
    size = channels // pieces
    copies = []
    for piece in range(pieces):
        for i in range(size):
            c = piece * size + i
            ready[c] = state[pl.ds(c * (rows + PAD), rows), :].astype(BF16)
        at = pl.ds(piece * size, size)
        copies.append(pltpu.make_async_copy(ready.at[at], out_hbm.at[at], sends.at[piece]))
        copies[-1].start()
    for each in copies:
        each.wait()


VMEM = pl.BlockSpec(memory_space=pltpu.VMEM)
HBM = pl.BlockSpec(memory_space=pltpu.HBM)


def local(field, land_mask, dw_weight, ln_gain, ln_shift, w_in, b_in, w_out):
    channels, rows, width = field.shape
    blocks = dw_weight.shape[0]
    tiles = channels * GROUP // width
    hidden = w_in.shape[1]
    flat = pltpu.VMEM((channels * (rows + PAD), width), F32)
    packed = pltpu.VMEM((blocks, 2, channels, width), BF16)
    tops = pltpu.VMEM((blocks, 3, channels, width), BF16)
    edges = pltpu.VMEM((blocks, rows // 2, width), BF16)
    wide = pltpu.VMEM((blocks, channels, width), F32)
    bands = pltpu.VMEM((blocks, channels * (rows + PAD), width), F32)
    args = (
        field,
        land_mask,
        jnp.swapaxes(dw_weight, 0, 1),
        ln_gain,
        ln_shift,
        jnp.swapaxes(w_in, 1, 2),
        b_in,
        w_out,
    )
    args = tuple(pltpu.with_memory_space_constraint(a, pltpu.HBM) for a in args)
    state = pl.pallas_call(
        functools.partial(kernel, lax.axis_size("zonal")),
        out_shape=flat,
        in_specs=[HBM] * 8,
        out_specs=VMEM,
        scratch_shapes=[pltpu.VMEM(a.shape, a.dtype) for a in args]
        + [
            flat,
            bands,
            bands,
            packed,
            tops,
            edges,
            packed,
            packed,
            tops,
            edges,
            edges,
            pltpu.VMEM((blocks, hidden, channels + 16), BF16),
            pltpu.VMEM((blocks, channels, hidden), BF16),
            wide,
            wide,
            pltpu.VMEM((2, width), F32),
            pltpu.VMEM((2, channels, width), F32),
            pltpu.VMEM((blocks, 21, channels, width), F32),
            pltpu.VMEM((blocks, 21, channels, width), F32),
            pltpu.VMEM((2 * width, 7 * width), BF16),
            pltpu.SemaphoreType.DMA((tiles + 7,)),
            pltpu.SemaphoreType.DMA((blocks, 7)),
            pltpu.SemaphoreType.DMA((blocks, 7)),
        ],
        compiler_params=pltpu.CompilerParams(
            collective_id=0, has_side_effects=True, vmem_limit_bytes=52 * 1024 * 1024
        ),
        name="evolve",
    )(*args)
    return pl.pallas_call(
        finish,
        out_shape=jax.ShapeDtypeStruct(field.shape, BF16),
        in_specs=[VMEM],
        out_specs=HBM,
        scratch_shapes=[
            pltpu.VMEM(field.shape, BF16),
            pltpu.SemaphoreType.DMA((2,)),
        ],
        compiler_params=pltpu.CompilerParams(vmem_limit_bytes=8 * 1024 * 1024),
        name="finish",
    )(state)


def solution(mesh):
    placed = (P("groups", None, "zonal"), P(None, "zonal"), P(), P(), P(), P(), P(), P())
    return jax.shard_map(
        local, mesh=mesh, in_specs=placed, out_specs=P("groups", None, "zonal"), check_vma=False
    )
```
